256 devices in a mesh: ta: 8 (over z), ha: 4 (over x_hi, core), wa: 8 (over x_lo, y).
Axes of the slice: x: 4 (x_hi: 2, x_lo: 2; x = x_hi * 2 + x_lo), y: 4, z: 8, core: 2. Of those that a mesh axis runs over, the one named last changes fastest.
Arguments:
- features: bfloat16 [32, 64, 128, 256], P('ta', 'ha', 'wa'), may hold values from -6 to 6
- norm_gain: float32 [256], replicated, may hold values from 0.5 to 1.5
- conv_weight: bfloat16 [3, 3, 3, 256, 256], replicated, may hold values from -0.078125 to 0.078125
- cotangent: bfloat16 [32, 64, 128, 256], P('ta', 'ha', 'wa'), may hold values from -6 to 6
Outputs:
- decoded: bfloat16 [32, 64, 128, 256], P('ta', 'ha', 'wa')
- grad_features: bfloat16 [32, 64, 128, 256], P('ta', 'ha', 'wa')
- grad_weight: float32 [3, 3, 3, 256, 256], P(None, None, None, None, ('ha', 'wa'))
The draws below stay inside these ranges and needn't reach their ends.
All inputs are finite; a program needn't handle non-finite values.
Results may differ from the reference program's by a relative error of at most 0.0032.
Values may be sent and summed in bfloat16 or wider, within the bound.
A program may use at most 128 MiB of HBM per device.

```python
import jax
import jax.numpy as jnp
from jax import lax

C = 256
FRAMES = 32
HEIGHT = 64
WIDTH = 128
VOXELS = 262144


def levels(rng, shape, cuts, low, high):
    factor_of, own = 1.0, jax.random.fold_in(rng, 6)
    for axis_at, blocks in cuts:
        draws = jnp.exp(jax.random.uniform(jax.random.fold_in(own, axis_at), (blocks,), jnp.float32, low / len(cuts), high / len(cuts)))
        factor_of = factor_of * jnp.repeat(draws, shape[axis_at] // blocks).reshape([-1 if axis == axis_at else 1 for axis in range(len(shape))])
    return factor_of


def normal_values(rng, shape, spread, reach, pieces=(), dtype=jnp.bfloat16):
    level = levels(rng, shape, pieces, -0.22, 0.18) if pieces else 1.0
    drawn = jax.random.normal(rng, shape, jnp.float32) * spread * level
    return jnp.minimum(jnp.maximum(drawn, -reach), reach).astype(dtype)


def setup_inputs(seed: int = 0) -> dict:
    streams_of = jax.random.split(jax.random.key(seed), 5)
    features = normal_values(streams_of[0], (FRAMES, HEIGHT, WIDTH, C), 1.0, 6.0, ((0, 8), (1, 4), (2, 8)))
    norm_gain = jnp.clip(jax.random.uniform(streams_of[1], (C,), jnp.float32, 0.5, 1.5), 0.5, 1.5)
    conv_weight = normal_values(streams_of[2], (3, 3, 3, C, C), (27 * C) ** -0.5, 0.078125)
    cotangent = normal_values(streams_of[3], (FRAMES, HEIGHT, WIDTH, C), 1.0, 6.0, ((0, 8), (1, 4), (2, 8)))
    return dict(features=features, norm_gain=norm_gain, conv_weight=conv_weight, cotangent=cotangent)


EPSILON = 1e-06

def activate(features, norm_gain):
    values = features.astype(jnp.float32)
    inverse = lax.rsqrt(lax.optimization_barrier(jnp.mean(values * values, axis=-1, keepdims=True)) + EPSILON)
    unit_rms = values * inverse
    normed = unit_rms * norm_gain
    activated = (normed * jax.nn.sigmoid(normed)).astype(jnp.bfloat16)
    return (values, inverse, unit_rms, normed, activated)

def norm_backward(grad_act, normed, unit_rms, inverse, norm_gain):
    logistic = jax.nn.sigmoid(normed)
    grad_normed = grad_act * logistic * (1.0 + normed * (1.0 - logistic))
    grad_unit = grad_normed * norm_gain
    return inverse * (grad_unit - unit_rms * lax.optimization_barrier(jnp.mean(grad_unit * unit_rms, axis=-1, keepdims=True)))

def reference(features, norm_gain, conv_weight, cotangent):
    frames, height, width, channels = features.shape
    values, inverse, unit_rms, normed, activated = activate(features, norm_gain)
    padded = jnp.pad(activated, ((2, 0), (1, 1), (1, 1), (0, 0))).astype(jnp.float32)
    kernel = conv_weight.astype(jnp.float32)
    grad_out = cotangent.astype(jnp.float32)
    flat_grad = grad_out.reshape(-1, channels)
    grad_padded = jnp.pad(grad_out, ((0, 2), (1, 1), (1, 1), (0, 0)))
    mixed = jnp.zeros((frames * height * width, channels), jnp.float32)
    grad_act = jnp.zeros((frames * height * width, channels), jnp.float32)
    weight_taps = []
    for t_off in range(3):
        for h_off in range(3):
            for w_off in range(3):
                window = padded[t_off:t_off + frames, h_off:h_off + height, w_off:w_off + width].reshape(-1, channels)
                mixed = mixed + jnp.dot(window, kernel[t_off, h_off, w_off], precision=lax.Precision.HIGHEST)
                weight_taps.append(lax.dot_general(window, flat_grad, (((0,), (0,)), ((), ())), precision=lax.Precision.HIGHEST))
                back = grad_padded[2 - t_off:2 - t_off + frames, 2 - h_off:2 - h_off + height, 2 - w_off:2 - w_off + width].reshape(-1, channels)
                grad_act = grad_act + jnp.dot(back, kernel[t_off, h_off, w_off].T, precision=lax.Precision.HIGHEST)
    grad_weight = jnp.stack(weight_taps).reshape(3, 3, 3, channels, channels) * VOXELS ** (-0.5)
    decoded = (values + mixed.reshape(features.shape)).astype(jnp.bfloat16)
    grad_norm = norm_backward(grad_act.reshape(features.shape), normed, unit_rms, inverse, norm_gain)
    grad_features = (grad_out + grad_norm).astype(jnp.bfloat16)
    return (decoded, grad_features, grad_weight)
```

```python
import jax
import jax.numpy as jnp
from jax import lax
from jax.experimental import pallas as pl
from jax.experimental.pallas import tpu as pltpu
from jax.sharding import PartitionSpec as P

EPSILON = 1e-06
MESH = pl.DeviceIdType.MESH
F32 = jnp.float32
BF16 = jnp.bfloat16
SLABS = 9
ROW = 18 * 16
PADDED = 6 * ROW
TICKS = 44


def dot(a, b):
    return jnp.dot(a, b, preferred_element_type=F32)


def wrap(value, count):
    return lax.rem(value + count, count)


def remote(src, dst, send, recv, device):
    return pltpu.make_async_remote_copy(
        src_ref=src, dst_ref=dst, send_sem=send, recv_sem=recv, device_id=device, device_id_type=MESH
    )


def normalise(cells, gain):
    values = cells.astype(F32)
    inverse = lax.rsqrt(jnp.mean(values * values, axis=-1, keepdims=True) + EPSILON)
    unit = values * inverse
    return values, inverse, unit, unit * gain


def kernel(
    scale,
    feat,
    gain,
    weight_hbm,
    cot,
    decoded,
    grad_feat,
    grad_weight,
    act,
    grd,
    act3,
    grd3,
    cot_t,
    weight,
    select,
    put_left,
    put_right,
    shift,
    edge,
    halo,
    mixed,
    back,
    part,
    pair,
    send1,
    recv1,
    mid,
    recv2,
    flat,
    recv3,
    total,
    weight_sem,
    halo_send,
    halo_recv,
    pair_sem,
    send1_sem,
    recv1_sem,
    send2_sem,
    recv2_sem,
    flat_sem,
    recv3_sem,
    total_send,
    total_recv,
):
    t = lax.axis_index("ta")
    ha = lax.axis_index("ha")
    wa = lax.axis_index("wa")
    core = lax.rem(ha, 2)
    x = (ha // 2) * 2 + wa // 4
    y = lax.rem(wa, 4)

    def at(z, xx, cc, yy):
        return (z, (xx // 2) * 2 + cc, lax.rem(xx, 2) * 4 + yy)

    def near(dt, dh, dw):
        return (wrap(t + dt, 8), wrap(ha + dh, 4), wrap(wa + dw, 8))

    partners = [near(0, 0, 1), near(0, 0, -1), near(0, 1, 0), near(0, -1, 0)]
    partners += [near(dt, dh, 0) for dt in (-1, 1) for dh in (-1, 1)]
    partners += [at(t, x, 1 - core, y)]
    partners += [at(t, wrap(x + k, 4), core, y) for k in (1, 2, 3)]
    partners += [at(t, x, core, wrap(y + k, 4)) for k in (1, 2, 3)]
    partners += [near(k, 0, 0) for k in range(1, 8)]
    barrier = pltpu.get_barrier_semaphore()
    for device in partners:
        pl.semaphore_signal(barrier, inc=1, device_id=device, device_id_type=MESH)

    load_weight = pltpu.make_async_copy(weight_hbm, weight, weight_sem)
    load_weight.start()

    @pl.loop(0, 16)
    def _(n):
        rows = pl.ds(pl.multiple_of(n * 64, 64), 64)
        normed = normalise(feat[rows, :], gain[...])[3]
        at_row = pl.multiple_of(((n // 4) * 18 + 1) * 16 + lax.rem(n, 4) * 64, 16)
        act[pl.ds(pl.multiple_of(at_row + 2 * ROW, 16), 64), :] = (normed * jax.nn.sigmoid(normed)).astype(BF16)
        grd[pl.ds(at_row, 64), :] = cot[rows, :]

    pl.semaphore_wait(barrier, len(partners))

    def block(ref, frame, frames, row, rows):
        return ref.at[pl.ds(frame, frames), pl.ds(row * 16, rows * 16), :]

    acts = act.reshape(6, ROW, 256)
    grds = grd.reshape(6, ROW, 256)
    first = []
    for n, (ref, dt, own, far) in enumerate(((acts, 1, 2, 0), (grds, -1, 0, 4))):
        edge_frame = 4 if dt == 1 else 0
        moves = [
            (near(dt, 0, 0), (edge_frame, 2, 1, 16), (far, 2, 1, 16)),
            (near(0, 1, 0), (own, 4, 16, 1), (own, 4, 0, 1)),
            (near(0, -1, 0), (own, 4, 1, 1), (own, 4, 17, 1)),
            (near(dt, 1, 0), (edge_frame, 2, 16, 1), (far, 2, 0, 1)),
            (near(dt, -1, 0), (edge_frame, 2, 1, 1), (far, 2, 17, 1)),
        ]
        first.append(
            [
                remote(block(ref, *src), block(ref, *dst), halo_send.at[n, m], halo_recv.at[n, m], device)
                for m, (device, src, dst) in enumerate(moves)
            ]
        )
    for copies in first:
        for copy in copies:
            copy.start()

    for n in range(4):
        cot_t[:, n * 256 : (n + 1) * 256] = cot[n * 256 : (n + 1) * 256, :].T

    def ones(condition):
        return jnp.where(condition, 1.0, 0.0).astype(BF16)

    cell = lax.broadcasted_iota(jnp.int32, (112, PADDED), 1)
    line = lax.broadcasted_iota(jnp.int32, (112, PADDED), 0) * 16
    select[0] = ones(cell == line + 15)
    select[1] = ones(cell == line)
    cell = lax.broadcasted_iota(jnp.int32, (PADDED, 112), 0)
    line = lax.broadcasted_iota(jnp.int32, (PADDED, 112), 1) * 16
    put_left[...] = ones(cell == line)
    put_right[...] = ones(cell == line + 15)
    cell = lax.broadcasted_iota(jnp.int32, (ROW, ROW), 0)
    other = lax.broadcasted_iota(jnp.int32, (ROW, ROW), 1)
    column = cell & 15
    shift[0] = ones((cell == other + 1) & (column != 0))
    shift[1] = ones((cell == other - 1) & (column != 15))

    second = []
    for n, (ref, refs, at_edge, edges) in enumerate(((act, acts, t == 0, (0, 1)), (grd, grds, t == 7, (4, 5)))):
        for copy in first[n]:
            copy.wait_recv()
        for copy in first[n]:
            copy.wait_send()

        @pl.when(at_edge)
        def _():
            for frame in edges:
                refs[frame] = jnp.zeros((ROW, 256), BF16)

        @pl.when(ha == 0)
        def _():
            for frame in range(6):
                refs[frame, 0:16, :] = jnp.zeros((16, 256), BF16)

        @pl.when(ha == 3)
        def _():
            for frame in range(6):
                refs[frame, 17 * 16 : ROW, :] = jnp.zeros((16, 256), BF16)

        copies = []
        for side in range(2):
            edge[n, side] = dot(select[side], ref[...]).astype(BF16)
            copy = remote(
                edge.at[n, side],
                halo.at[n, side],
                halo_send.at[n, 5 + side],
                halo_recv.at[n, 5 + side],
                near(0, 0, 1 if side == 0 else -1),
            )
            copy.start()
            copies.append(copy)
        second.append(copies)

    for n, (ref, wide) in enumerate(((act, act3), (grd, grd3))):
        wide[:, 256:512] = ref[...]
        for copy in second[n]:
            copy.wait_recv()

        @pl.when(wa == 0)
        def _():
            halo[n, 0] = jnp.zeros((112, 256), BF16)

        @pl.when(wa == 7)
        def _():
            halo[n, 1] = jnp.zeros((112, 256), BF16)

        for side, put, lanes in ((0, put_left, 0), (1, put_right, 512)):

            @pl.loop(0, 6)
            def _(frame):
                rows = pl.ds(pl.multiple_of(frame * ROW, 16), ROW)
                moved = dot(shift[side], ref[rows, :]) + dot(put[rows, :], halo[n, side])
                wide[rows, lanes : lanes + 256] = moved.astype(BF16)

        for copy in second[n]:
            copy.wait_send()

    load_weight.wait()
    mixed[...] = jnp.zeros_like(mixed)
    back[...] = jnp.zeros_like(back)

    def to_pair(s):
        return remote(
            part.at[s, :, 1 - core], pair.at[s], pair_sem.at[0, s], pair_sem.at[1, s], at(t, x, 1 - core, y)
        )

    def along(half, k):
        return at(t, wrap(x + k, 4), core, y) if half == 0 else at(t, x, core, wrap(y + k, 4))

    def copy1(s, half, k):
        slot = wrap((x if half == 0 else y) + k, 4)
        return remote(
            send1.at[s, half, slot],
            recv1.at[s, half, k - 1],
            send1_sem.at[s, half, k - 1],
            recv1_sem.at[s, half, k - 1],
            along(half, k),
        )

    def copy2(s, half, k):
        slot = wrap((y if half == 0 else x) + k, 4)
        return remote(
            mid.at[s, half, slot],
            recv2.at[s, half, k - 1],
            send2_sem.at[s, half, k - 1],
            recv2_sem.at[s, half, k - 1],
            along(1 - half, k),
        )

    def stage_gradient(s):
        i, j = s // 3, lax.rem(s, 3)
        acc = None
        for n in range(4):
            rows = pl.ds(pl.multiple_of((n + i) * ROW + j * 16, 16), 256)
            term = dot(cot_t[:, n * 256 : (n + 1) * 256], act3[rows, :])
            acc = term if acc is None else acc + term
        part[s] = acc.reshape(2, 2, 64, 768)
        to_pair(s).start()

    def stage_first(s):
        to_pair(s).wait_recv()
        for n in range(2):
            pair[s, n] = pair[s, n] + part[s, n, core]
        for d in range(4):
            n, r = d // 2, (d % 2) * 32
            send1[s, 0, d] = pair[s, n, r : r + 32, 0:384].astype(BF16)
            rows = [pair[s, e // 2, (e % 2) * 32 + d * 8 : (e % 2) * 32 + d * 8 + 8, 384:768] for e in range(4)]
            send1[s, 1, d] = jnp.concatenate(rows, axis=0).astype(BF16)
        for k in (2, 1, 3):
            for half in range(2):
                copy1(s, half, k).start()

    def stage_second(s):
        for half in range(2):
            for k in (1, 2, 3):
                copy1(s, half, k).wait_recv()
        own = pair[s, x // 2, pl.ds(pl.multiple_of(lax.rem(x, 2) * 32, 32), 32), 0:384]
        for k in range(3):
            own = own + recv1[s, 0, k].astype(F32)
        mid[s, 0] = own.reshape(4, 8, 384)
        rows = [
            pair[s, e // 2, pl.ds(pl.multiple_of((e % 2) * 32 + y * 8, 8), 8), 384:768] for e in range(4)
        ]
        own = jnp.concatenate(rows, axis=0)
        for k in range(3):
            own = own + recv1[s, 1, k].astype(F32)
        mid[s, 1] = own.reshape(4, 8, 384)
        for k in (2, 1, 3):
            for half in range(2):
                copy2(s, half, k).start()

    def owner_of(s):
        return lax.rem(s, 8)

    def to_owner(s):
        k = wrap(t - owner_of(s) - 1, 8)
        return remote(
            flat.at[s], recv3.at[s // 8, k], flat_sem.at[s], recv3_sem.at[s // 8, k], (owner_of(s), ha, wa)
        )

    def from_owner(s, k):
        return remote(
            total.at[s],
            total.at[s],
            total_send.at[s // 8, k - 1],
            total_recv.at[s],
            (wrap(t + k, 8), ha, wa),
        )

    def stage_third(s):
        for half in range(2):
            for k in (1, 2, 3):
                copy2(s, half, k).wait_recv()
        for half, slot in ((0, y), (1, x)):
            own = mid[s, half, slot]
            for k in range(3):
                own = own + recv2[s, half, k]
            flat[s, :, half * 384 : half * 384 + 384] = own

        @pl.when(t != owner_of(s))
        def _():
            to_owner(s).start()

    def stage_owner(s):
        @pl.when(t == owner_of(s))
        def _():
            for k in range(7):
                remote(
                    flat.at[s], recv3.at[s // 8, k], flat_sem.at[s], recv3_sem.at[s // 8, k], near(1, 0, 0)
                ).wait_recv()
            own = flat[s]
            for k in range(7):
                own = own + recv3[s // 8, k]
            own = own * scale
            for k in range(3):
                total[s, k] = own[:, k * 256 : k * 256 + 256]
            for k in (4, 3, 5, 2, 6, 1, 7):
                from_owner(s, k).start()

    def stage_mixed(s):
        i, j = s // 3, lax.rem(s, 3)
        for n in range(4):
            rows = pl.ds(pl.multiple_of((n + i) * ROW + j * 16, 16), 256)
            mixed[n * 256 : n * 256 + 256, :] += dot(act3[rows, :], weight[s])

    def stage_back(s):
        i, j = s // 3, lax.rem(s, 3)
        for n in range(4):
            rows = pl.ds(pl.multiple_of((n + 2 - i) * ROW + (2 - j) * 16, 16), 256)
            acc = None
            for k in range(3):
                term = lax.dot_general(
                    grd3[rows, (2 - k) * 256 : (3 - k) * 256],
                    weight[s, k * 256 : k * 256 + 256, :],
                    (((1,), (1,)), ((), ())),
                    preferred_element_type=F32,
                )
                acc = term if acc is None else acc + term
            back[n * 256 : n * 256 + 256, :] += acc

    plan = (
        (stage_gradient, 0, 1),
        (stage_first, 2, 1),
        (stage_second, 8, 2),
        (stage_third, 13, 2),
        (stage_owner, 19, 2),
        (stage_mixed, 9, 1),
        (stage_back, 18, 1),
    )

    @pl.loop(0, TICKS)
    def _(tick):
        for stage, begin, step in plan:
            s = (tick - begin) // step

            @pl.when((tick >= begin) & (s < SLABS) & (lax.rem(tick - begin + 64, step) == 0))
            def _():
                stage(s)

    @pl.loop(0, 16)
    def _(n):
        rows = pl.ds(pl.multiple_of(n * 64, 64), 64)
        values, inverse, unit, normed = normalise(feat[rows, :], gain[...])
        decoded[rows, :] = (values + mixed[rows, :]).astype(BF16)
        logistic = jax.nn.sigmoid(normed)
        grad_unit = back[rows, :] * logistic * (1.0 + normed * (1.0 - logistic)) * gain[...]
        grad = inverse * (grad_unit - unit * jnp.mean(grad_unit * unit, axis=-1, keepdims=True))
        grad_feat[rows, :] = (cot[rows, :].astype(F32) + grad).astype(BF16)

    @pl.loop(0, SLABS)
    def _(s):
        to_pair(s).wait_send()
        for half in range(2):
            for k in (1, 2, 3):
                copy1(s, half, k).wait_send()
                copy2(s, half, k).wait_send()

        @pl.when(t != owner_of(s))
        def _():
            to_owner(s).wait_send()
            from_owner(s, 1).wait_recv()

        @pl.when(t == owner_of(s))
        def _():
            for k in range(1, 8):
                from_owner(s, k).wait_send()

        for k in range(3):
            grad_weight[s * 3 + k] = total[s, k]


def body(features, norm_gain, conv_weight, cotangent):
    frames, height, width, channels = features.shape
    cells = frames * height * width
    owners = lax.axis_size("ha") * lax.axis_size("wa")
    voxels = cells * owners * lax.axis_size("ta")
    vmem = pl.BlockSpec(memory_space=pltpu.VMEM)
    dma = pltpu.SemaphoreType.DMA

    def run(*refs):
        kernel(float(voxels) ** (-0.5), *refs)

    decoded, grad_features, grad_weight = pl.pallas_call(
        run,
        out_shape=(
            jax.ShapeDtypeStruct((cells, channels), BF16),
            jax.ShapeDtypeStruct((cells, channels), BF16),
            jax.ShapeDtypeStruct((27, channels // owners, channels), F32),
        ),
        in_specs=[vmem, vmem, pl.BlockSpec(memory_space=pl.ANY), vmem],
        out_specs=(vmem, vmem, vmem),
        scratch_shapes=[
            pltpu.VMEM((PADDED, 256), BF16),
            pltpu.VMEM((PADDED, 256), BF16),
            pltpu.VMEM((PADDED, 768), BF16),
            pltpu.VMEM((PADDED, 768), BF16),
            pltpu.VMEM((256, 1024), BF16),
            pltpu.VMEM((SLABS, 768, 256), BF16),
            pltpu.VMEM((2, 112, PADDED), BF16),
            pltpu.VMEM((PADDED, 112), BF16),
            pltpu.VMEM((PADDED, 112), BF16),
            pltpu.VMEM((2, ROW, ROW), BF16),
            pltpu.VMEM((2, 2, 112, 256), BF16),
            pltpu.VMEM((2, 2, 112, 256), BF16),
            pltpu.VMEM((1024, 256), F32),
            pltpu.VMEM((1024, 256), F32),
            pltpu.VMEM((SLABS, 2, 2, 64, 768), F32),
            pltpu.VMEM((SLABS, 2, 64, 768), F32),
            pltpu.VMEM((SLABS, 2, 4, 32, 384), BF16),
            pltpu.VMEM((SLABS, 2, 3, 32, 384), BF16),
            pltpu.VMEM((SLABS, 2, 4, 8, 384), F32),
            pltpu.VMEM((SLABS, 2, 3, 8, 384), F32),
            pltpu.VMEM((SLABS, 8, 768), F32),
            pltpu.VMEM((2, 7, 8, 768), F32),
            pltpu.VMEM((SLABS, 3, 8, 256), F32),
            dma,
            dma((2, 7)),
            dma((2, 7)),
            dma((2, SLABS)),
            dma((SLABS, 2, 3)),
            dma((SLABS, 2, 3)),
            dma((SLABS, 2, 3)),
            dma((SLABS, 2, 3)),
            dma((SLABS,)),
            dma((2, 7)),
            dma((2, 7)),
            dma((SLABS,)),
        ],
        compiler_params=pltpu.CompilerParams(
            collective_id=0, has_side_effects=True, vmem_limit_bytes=60 << 20
        ),
    )(
        features.reshape(cells, channels),
        norm_gain.reshape(1, channels),
        conv_weight.reshape(9, 3 * channels, channels),
        cotangent.reshape(cells, channels),
    )
    grad_weight = grad_weight.reshape(3, 3, 3, channels // owners, channels).transpose(0, 1, 2, 4, 3)
    return decoded.reshape(features.shape), grad_features.reshape(features.shape), grad_weight


def solution(mesh):
    placed = (P("ta", "ha", "wa", None), P(), P(), P("ta", "ha", "wa", None))
    return jax.shard_map(
        body,
        mesh=mesh,
        in_specs=placed,
        out_specs=(
            P("ta", "ha", "wa", None),
            P("ta", "ha", "wa", None),
            P(None, None, None, None, ("ha", "wa")),
        ),
        check_vma=False,
    )
```

```python
import jax
import jax.numpy as jnp
from jax import lax
from jax.experimental import pallas as pl
from jax.experimental.pallas import tpu as pltpu
from jax.sharding import PartitionSpec as P

EPSILON = 1e-06
MESH = pl.DeviceIdType.MESH
F32 = jnp.float32
BF16 = jnp.bfloat16
SLABS = 9
ROW = 18 * 16
PADDED = 6 * ROW
TICKS = 38


def dot(a, b):
    return jnp.dot(a, b, preferred_element_type=F32)


def wrap(value, count):
    return lax.rem(value + count, count)


def remote(src, dst, send, recv, device):
    return pltpu.make_async_remote_copy(
        src_ref=src, dst_ref=dst, send_sem=send, recv_sem=recv, device_id=device, device_id_type=MESH
    )


def normalise(cells, gain):
    values = cells.astype(F32)
    inverse = lax.rsqrt(jnp.mean(values * values, axis=-1, keepdims=True) + EPSILON)
    unit = values * inverse
    return values, inverse, unit, unit * gain


def kernel(
    scale,
    feat_hbm,
    gain,
    weight_hbm,
    cot_hbm,
    decoded,
    grad_feat,
    grad_weight,
    feat,
    cot,
    act,
    grd,
    act3,
    grd3,
    cot_t,
    weight,
    select,
    put,
    shift,
    edge,
    halo,
    halo_t,
    mixed,
    back,
    part,
    pair,
    send1,
    recv1,
    mid,
    recv2,
    flat,
    recv3,
    total,
    load_sem,
    halo_send,
    halo_recv,
    pair_sem,
    send1_sem,
    recv1_sem,
    send2_sem,
    recv2_sem,
    flat_sem,
    recv3_sem,
    total_send,
    total_recv,
):
    t = lax.axis_index("ta")
    ha = lax.axis_index("ha")
    wa = lax.axis_index("wa")
    core = lax.rem(ha, 2)
    x = (ha // 2) * 2 + wa // 4
    y = lax.rem(wa, 4)

    def at(z, xx, cc, yy):
        return (z, (xx // 2) * 2 + cc, lax.rem(xx, 2) * 4 + yy)

    def near(dt, dh, dw):
        return (wrap(t + dt, 8), wrap(ha + dh, 4), wrap(wa + dw, 8))

    partners = [near(0, dh, dw) for dh in (-1, 0, 1) for dw in (-1, 0, 1) if (dh, dw) != (0, 0)]
    partners += [at(t, x, 1 - core, y)]
    partners += [at(t, wrap(x + k, 4), core, y) for k in (1, 2, 3)]
    partners += [at(t, x, core, wrap(y + k, 4)) for k in (1, 2, 3)]
    partners += [near(k, 0, 0) for k in range(1, 8)]
    barrier = pltpu.get_barrier_semaphore()
    for device in partners:
        pl.semaphore_signal(barrier, inc=1, device_id=device, device_id_type=MESH)

    loads = [
        pltpu.make_async_copy(far, here, load_sem.at[n])
        for n, (far, here) in enumerate(((feat_hbm, feat), (cot_hbm, cot), (weight_hbm, weight)))
    ]
    for load in loads:
        load.start()

    def ones(condition):
        return jnp.where(condition, 1.0, 0.0).astype(BF16)

    line = lax.broadcasted_iota(jnp.int32, (96, 1024), 0)
    cell = lax.broadcasted_iota(jnp.int32, (96, 1024), 1)
    first_column = jnp.where(line < 64, line * 16, (line & 15) * 256 + jnp.where(line < 80, 240, 0))
    usable = (line < 64) | ((line & 15) < 4)
    select[0] = ones(usable & (cell == first_column + 15))
    select[1] = ones(usable & (cell == first_column))
    for n in range(4):
        line = lax.broadcasted_iota(jnp.int32, (ROW, 96), 1)
        cell = lax.broadcasted_iota(jnp.int32, (ROW, 96), 0)
        row = jnp.where(line < 64, (line & 15) + 1, jnp.where(line < 80, 0, 17))
        frame = jnp.where(line < 64, line // 16, line & 15)
        put[0, n] = ones((frame == n) & (cell == row * 16))
        put[1, n] = ones((frame == n) & (cell == row * 16 + 15))
    cell = lax.broadcasted_iota(jnp.int32, (ROW, ROW), 0)
    other = lax.broadcasted_iota(jnp.int32, (ROW, ROW), 1)
    column = cell & 15
    shift[0] = ones((cell == other + 1) & (column != 0))
    shift[1] = ones((cell == other - 1) & (column != 15))

    loads[0].wait()

    @pl.loop(0, 16)
    def _(n):
        rows = pl.ds(pl.multiple_of(n * 64, 64), 64)
        normed = normalise(feat[rows, :], gain[...])[3]
        act[2 + n // 4, pl.ds(pl.multiple_of(lax.rem(n, 4) * 64 + 16, 16), 64), :] = (
            normed * jax.nn.sigmoid(normed)
        ).astype(BF16)

    loads[1].wait()
    for n in range(4):
        grd[n, 16:272, :] = cot[n * 256 : n * 256 + 256, :]
    for n, (ref, own) in enumerate(((act, 2), (grd, 0))):
        for side in range(2):
            acc = None
            for f in range(4):
                term = dot(select[side, :, f * 256 : f * 256 + 256], ref[own + f, 16:272, :])
                acc = term if acc is None else acc + term
            edge[n, side] = acc.astype(BF16)

    pl.semaphore_wait(barrier, len(partners))

    def rows_of(ref, frame, frames, row, rows):
        return ref.at[pl.ds(frame, frames), pl.ds(row * 16, rows * 16), :]

    first = []
    early = []
    late = []
    for n, (ref, dt, own, ends) in enumerate(((act, 1, 2, ((5, 1), (4, 0))), (grd, -1, 0, ((0, 4), (1, 5))))):
        at_sem = iter(range(13))

        def move(source, target, device):
            m = next(at_sem)
            return remote(source, target, halo_send.at[n, m], halo_recv.at[n, m], device)

        moves = [
            move(rows_of(ref, own, 4, 16, 1), rows_of(ref, own, 4, 0, 1), near(0, 1, 0)),
            move(rows_of(ref, own, 4, 1, 1), rows_of(ref, own, 4, 17, 1), near(0, -1, 0)),
        ]
        for side, dw in ((0, 1), (1, -1)):
            for begin, count, dh in ((0, 64, 0), (64, 16, 1), (80, 16, -1)):
                lines = pl.ds(begin, count)
                moves.append(move(edge.at[n, side, lines], halo.at[n, side, lines], near(0, dh, dw)))
        first.append(moves)
        early.append([move(rows_of(ref, a, 1, 1, 16), rows_of(ref, b, 1, 1, 16), near(dt, 0, 0)) for a, b in ends])
        (a0, b0), (a1, b1) = ends
        a, b = min(a0, a1), min(b0, b1)
        late.append(
            [move(rows_of(ref, a, 2, row, 1), rows_of(ref, b, 2, row, 1), near(dt, 0, 0)) for row in (0, 17)]
            + [move(halo.at[n], halo_t.at[n], near(dt, 0, 0))]
        )
    for group in (first[0], early[0], first[1], early[1]):
        for copy in group:
            copy.start()

    for n in range(4):
        cot_t[:, n * 256 : (n + 1) * 256] = cot[n * 256 : (n + 1) * 256, :].T
    mixed[...] = jnp.zeros_like(mixed)
    back[...] = jnp.zeros_like(back)
    loads[2].wait()

    def take_first(n, ref, own):
        for copy in first[n]:
            copy.wait_recv()
        for copy in first[n]:
            copy.wait_send()

        @pl.when(ha == 0)
        def _():
            for frame in range(4):
                ref[own + frame, 0:16, :] = jnp.zeros((16, 256), BF16)
            for side in range(2):
                halo[n, side, 64:80] = jnp.zeros((16, 256), BF16)

        @pl.when(ha == 3)
        def _():
            for frame in range(4):
                ref[own + frame, 272:288, :] = jnp.zeros((16, 256), BF16)
            for side in range(2):
                halo[n, side, 80:96] = jnp.zeros((16, 256), BF16)

        @pl.when(wa == 0)
        def _():
            halo[n, 0] = jnp.zeros((96, 256), BF16)

        @pl.when(wa == 7)
        def _():
            halo[n, 1] = jnp.zeros((96, 256), BF16)

        for copy in late[n]:
            copy.start()

    def take_late(n, ref, far, at_end):
        for copy in early[n] + late[n]:
            copy.wait_recv()
        for copy in early[n] + late[n]:
            copy.wait_send()

        @pl.when(at_end)
        def _():
            for frame in (far, far + 1):
                ref[frame] = jnp.zeros((ROW, 256), BF16)
            for side in range(2):
                halo_t[n, side] = jnp.zeros((96, 256), BF16)

    def widen(n, ref, wide, frame, own, borders):
        rows = pl.ds(pl.multiple_of(frame * ROW, 16), ROW)
        wide[rows, 256:512] = ref[frame]
        for side, lanes in ((0, 0), (1, 512)):
            moved = dot(shift[side], ref[frame]) + dot(put[side, own], borders[n, side])
            wide[rows, lanes : lanes + 256] = moved.astype(BF16)

    take_first(0, act, 2)

    @pl.loop(0, 4)
    def _(frame):
        widen(0, act, act3, frame + 2, frame, halo)

    def to_pair(s):
        return remote(
            part.at[s, :, 1 - core], pair.at[s], pair_sem.at[0, s], pair_sem.at[1, s], at(t, x, 1 - core, y)
        )

    def along(half, k):
        return at(t, wrap(x + k, 4), core, y) if half == 0 else at(t, x, core, wrap(y + k, 4))

    def copy1(s, half, k):
        slot = wrap((x if half == 0 else y) + k, 4)
        return remote(
            send1.at[s, half, slot],
            recv1.at[s, half, k - 1],
            send1_sem.at[s, half, k - 1],
            recv1_sem.at[s, half, k - 1],
            along(half, k),
        )

    def copy2(s, half, k):
        slot = wrap((y if half == 0 else x) + k, 4)
        return remote(
            mid.at[s, half, slot],
            recv2.at[s, half, k - 1],
            send2_sem.at[s, half, k - 1],
            recv2_sem.at[s, half, k - 1],
            along(1 - half, k),
        )

    def stage_gradient(s):
        i, j = 2 - s // 3, lax.rem(s, 3)
        acc = None
        for n in range(4):
            rows = pl.ds(pl.multiple_of((n + i) * ROW + j * 16, 16), 256)
            term = dot(cot_t[:, n * 256 : (n + 1) * 256], act3[rows, :])
            acc = term if acc is None else acc + term
        part[s] = acc.reshape(2, 2, 64, 768)
        to_pair(s).start()

    def stage_first(s):
        to_pair(s).wait_recv()
        for n in range(2):
            pair[s, n] = pair[s, n] + part[s, n, core]
        for d in range(4):
            n, r = d // 2, (d % 2) * 32
            send1[s, 0, d] = pair[s, n, r : r + 32, 0:384].astype(BF16)
            rows = [pair[s, e // 2, (e % 2) * 32 + d * 8 : (e % 2) * 32 + d * 8 + 8, 384:768] for e in range(4)]
            send1[s, 1, d] = jnp.concatenate(rows, axis=0).astype(BF16)
        for k in (2, 1, 3):
            for half in range(2):
                copy1(s, half, k).start()

    def stage_second(s):
        for half in range(2):
            for k in (1, 2, 3):
                copy1(s, half, k).wait_recv()
        own = pair[s, x // 2, pl.ds(pl.multiple_of(lax.rem(x, 2) * 32, 32), 32), 0:384]
        for k in range(3):
            own = own + recv1[s, 0, k].astype(F32)
        mid[s, 0] = own.reshape(4, 8, 384)
        rows = [
            pair[s, e // 2, pl.ds(pl.multiple_of((e % 2) * 32 + y * 8, 8), 8), 384:768] for e in range(4)
        ]
        own = jnp.concatenate(rows, axis=0)
        for k in range(3):
            own = own + recv1[s, 1, k].astype(F32)
        mid[s, 1] = own.reshape(4, 8, 384)
        for k in (2, 1, 3):
            for half in range(2):
                copy2(s, half, k).start()

    def owner_of(s):
        return lax.rem(s, 8)

    def to_owner(s):
        k = wrap(t - owner_of(s) - 1, 8)
        return remote(
            flat.at[s], recv3.at[s // 8, k], flat_sem.at[s], recv3_sem.at[s // 8, k], (owner_of(s), ha, wa)
        )

    def from_owner(s, k):
        return remote(
            total.at[s],
            total.at[s],
            total_send.at[s // 8, k - 1],
            total_recv.at[s],
            (wrap(t + k, 8), ha, wa),
        )

    def stage_third(s):
        for half in range(2):
            for k in (1, 2, 3):
                copy2(s, half, k).wait_recv()
        for half, slot in ((0, y), (1, x)):
            own = mid[s, half, slot]
            for k in range(3):
                own = own + recv2[s, half, k]
            flat[s, :, half * 384 : half * 384 + 384] = own

        @pl.when(t != owner_of(s))
        def _():
            to_owner(s).start()

    def stage_owner(s):
        @pl.when(t == owner_of(s))
        def _():
            for k in range(7):
                remote(
                    flat.at[s], recv3.at[s // 8, k], flat_sem.at[s], recv3_sem.at[s // 8, k], near(1, 0, 0)
                ).wait_recv()
            own = flat[s]
            for k in range(7):
                own = own + recv3[s // 8, k]
            own = own * scale
            for k in range(3):
                total[s, k] = own[:, k * 256 : k * 256 + 256]
            for k in (4, 3, 5, 2, 6, 1, 7):
                from_owner(s, k).start()

    def stage_mixed(s):
        i, j = s // 3, lax.rem(s, 3)
        for n in range(4):
            rows = pl.ds(pl.multiple_of((n + i) * ROW + j * 16, 16), 256)
            mixed[n * 256 : n * 256 + 256, :] += dot(act3[rows, :], weight[s])

    def stage_back(s):
        i, j = s // 3, lax.rem(s, 3)
        for n in range(4):
            rows = pl.ds(pl.multiple_of((n + 2 - i) * ROW + (2 - j) * 16, 16), 256)
            acc = None
            for k in range(3):
                term = lax.dot_general(
                    grd3[rows, (2 - k) * 256 : (3 - k) * 256],
                    weight[s, k * 256 : k * 256 + 256, :],
                    (((1,), (1,)), ((), ())),
                    preferred_element_type=F32,
                )
                acc = term if acc is None else acc + term
            back[n * 256 : n * 256 + 256, :] += acc

    def stage_act(_):
        take_late(0, act, 0, t == 0)
        for frame in range(2):
            widen(0, act, act3, frame, frame + 2, halo_t)
        take_first(1, grd, 0)

    def stage_cot(frame):
        widen(1, grd, grd3, frame, frame, halo)

    def stage_cot_late(_):
        take_late(1, grd, 4, t == 7)
        for frame in range(2):
            widen(1, grd, grd3, frame + 4, frame, halo_t)

    def stage_decoded(n):
        for m in range(4):
            rows = pl.ds(pl.multiple_of(n * 256 + m * 64, 64), 64)
            decoded[rows, :] = (feat[rows, :].astype(F32) + mixed[rows, :]).astype(BF16)

    def stage_grad(n):
        @pl.loop(0, 4)
        def _(m):
            rows = pl.ds(pl.multiple_of(n * 256 + m * 64, 64), 64)
            _, inverse, unit, normed = normalise(feat[rows, :], gain[...])
            logistic = jax.nn.sigmoid(normed)
            grad_unit = back[rows, :] * logistic * (1.0 + normed * (1.0 - logistic)) * gain[...]
            grad = inverse * (grad_unit - unit * jnp.mean(grad_unit * unit, axis=-1, keepdims=True))
            grad_feat[rows, :] = (cot[rows, :].astype(F32) + grad).astype(BF16)

    plan = (
        (stage_act, 3, 1, 1),
        (stage_gradient, 0, 1, SLABS),
        (stage_first, 2, 1, SLABS),
        (stage_second, 8, 2, SLABS),
        (stage_third, 13, 2, SLABS),
        (stage_owner, 20, 2, SLABS),
        (stage_mixed, 9, 1, SLABS),
        (stage_cot, 9, 1, 4),
        (stage_cot_late, 14, 1, 1),
        (stage_back, 18, 1, SLABS),
        (stage_decoded, 19, 2, 4),
        (stage_grad, 27, 1, 4),
    )

    @pl.loop(0, TICKS)
    def _(tick):
        for stage, begin, step, count in plan:
            s = (tick - begin) // step

            @pl.when((tick >= begin) & (tick < begin + step * count) & (lax.rem(tick - begin + 64, step) == 0))
            def _():
                stage(s)

    @pl.loop(0, SLABS)
    def _(s):
        to_pair(s).wait_send()
        for half in range(2):
            for k in (1, 2, 3):
                copy1(s, half, k).wait_send()
                copy2(s, half, k).wait_send()

        @pl.when(t != owner_of(s))
        def _():
            to_owner(s).wait_send()
            from_owner(s, 1).wait_recv()

        @pl.when(t == owner_of(s))
        def _():
            for k in range(1, 8):
                from_owner(s, k).wait_send()

        for k in range(3):
            grad_weight[(2 - s // 3) * 9 + lax.rem(s, 3) * 3 + k] = total[s, k]


def finish(*refs):
    copies = [pltpu.make_async_copy(refs[n], refs[n + 3], refs[6].at[n]) for n in range(3)]
    for copy in copies:
        copy.start()
    for copy in copies:
        copy.wait()


def body(features, norm_gain, conv_weight, cotangent):
    frames, height, width, channels = features.shape
    cells = frames * height * width
    owners = lax.axis_size("ha") * lax.axis_size("wa")
    voxels = cells * owners * lax.axis_size("ta")
    vmem = pl.BlockSpec(memory_space=pltpu.VMEM)
    hbm = pl.BlockSpec(memory_space=pltpu.HBM)
    anywhere = pl.BlockSpec(memory_space=pl.ANY)
    dma = pltpu.SemaphoreType.DMA

    def run(*refs):
        kernel(float(voxels) ** (-0.5), *refs)

    results = (
        jax.ShapeDtypeStruct((cells, channels), BF16),
        jax.ShapeDtypeStruct((cells, channels), BF16),
        jax.ShapeDtypeStruct((27, channels // owners, channels), F32),
    )
    held = pl.pallas_call(
        run,
        out_shape=results,
        in_specs=[hbm, vmem, hbm, hbm],
        out_specs=(vmem, vmem, vmem),
        scratch_shapes=[
            pltpu.VMEM((1024, 256), BF16),
            pltpu.VMEM((1024, 256), BF16),
            pltpu.VMEM((6, ROW, 256), BF16),
            pltpu.VMEM((6, ROW, 256), BF16),
            pltpu.VMEM((PADDED, 768), BF16),
            pltpu.VMEM((PADDED, 768), BF16),
            pltpu.VMEM((256, 1024), BF16),
            pltpu.VMEM((SLABS, 768, 256), BF16),
            pltpu.VMEM((2, 96, 1024), BF16),
            pltpu.VMEM((2, 4, ROW, 96), BF16),
            pltpu.VMEM((2, ROW, ROW), BF16),
            pltpu.VMEM((2, 2, 96, 256), BF16),
            pltpu.VMEM((2, 2, 96, 256), BF16),
            pltpu.VMEM((2, 2, 96, 256), BF16),
            pltpu.VMEM((1024, 256), F32),
            pltpu.VMEM((1024, 256), F32),
            pltpu.VMEM((SLABS, 2, 2, 64, 768), F32),
            pltpu.VMEM((SLABS, 2, 64, 768), F32),
            pltpu.VMEM((SLABS, 2, 4, 32, 384), BF16),
            pltpu.VMEM((SLABS, 2, 3, 32, 384), BF16),
            pltpu.VMEM((SLABS, 2, 4, 8, 384), F32),
            pltpu.VMEM((SLABS, 2, 3, 8, 384), F32),
            pltpu.VMEM((SLABS, 8, 768), F32),
            pltpu.VMEM((2, 7, 8, 768), F32),
            pltpu.VMEM((SLABS, 3, 8, 256), F32),
            dma((3,)),
            dma((2, 13)),
            dma((2, 13)),
            dma((2, SLABS)),
            dma((SLABS, 2, 3)),
            dma((SLABS, 2, 3)),
            dma((SLABS, 2, 3)),
            dma((SLABS, 2, 3)),
            dma((SLABS,)),
            dma((2, 7)),
            dma((2, 7)),
            dma((SLABS,)),
        ],
        compiler_params=pltpu.CompilerParams(
            collective_id=0, has_side_effects=True, vmem_limit_bytes=52 << 20
        ),
    )(
        features.reshape(cells, channels),
        norm_gain.reshape(1, channels),
        conv_weight.reshape(9, 3 * channels, channels),
        cotangent.reshape(cells, channels),
    )
    decoded, grad_features, grad_weight = pl.pallas_call(
        finish,
        out_shape=results,
        in_specs=[anywhere] * 3,
        out_specs=[hbm] * 3,
        scratch_shapes=[dma((3,))],
        compiler_params=pltpu.CompilerParams(vmem_limit_bytes=4 << 20),
    )(*held)
    grad_weight = grad_weight.reshape(3, 3, 3, channels // owners, channels).transpose(0, 1, 2, 4, 3)
    return decoded.reshape(features.shape), grad_features.reshape(features.shape), grad_weight


def solution(mesh):
    placed = (P("ta", "ha", "wa", None), P(), P(), P("ta", "ha", "wa", None))
    return jax.shard_map(
        body,
        mesh=mesh,
        in_specs=placed,
        out_specs=(
            P("ta", "ha", "wa", None),
            P("ta", "ha", "wa", None),
            P(None, None, None, None, ("ha", "wa")),
        ),
        check_vma=False,
    )
```

```python
import jax
import jax.numpy as jnp
from jax import lax
from jax.experimental import pallas as pl
from jax.experimental.pallas import tpu as pltpu
from jax.sharding import PartitionSpec as P

EPSILON = 1e-06
MESH = pl.DeviceIdType.MESH
F32 = jnp.float32
BF16 = jnp.bfloat16
SLABS = 9
OWNED = 8
ROW = 18 * 16
PADDED = 6 * ROW
TICKS = 34


def dot(a, b):
    return jnp.dot(a, b, preferred_element_type=F32)


def wrap(value, count):
    return lax.rem(value + count, count)


def remote(src, dst, send, recv, device):
    return pltpu.make_async_remote_copy(
        src_ref=src, dst_ref=dst, send_sem=send, recv_sem=recv, device_id=device, device_id_type=MESH
    )


def normalise(cells, gain):
    values = cells.astype(F32)
    inverse = lax.rsqrt(jnp.mean(values * values, axis=-1, keepdims=True) + EPSILON)
    unit = values * inverse
    return values, inverse, unit, unit * gain


def kernel(
    scale,
    feat_hbm,
    gain_hbm,
    weight_hbm,
    cot_hbm,
    decoded,
    grad_feat,
    grad_weight,
    gain,
    feat,
    cot,
    act,
    grd,
    act3,
    grd3,
    cot_t,
    weight,
    select,
    put,
    shift,
    edge,
    halo,
    halo_t,
    mixed,
    back,
    part,
    pair,
    send1,
    recv1,
    mid,
    send2,
    recv2,
    flat,
    recv3,
    every,
    total,
    load_sem,
    halo_send,
    halo_recv,
    pair_sem,
    send1_sem,
    recv1_sem,
    send2_sem,
    recv2_sem,
    flat_sem,
    recv3_sem,
    every_send,
    every_recv,
    total_send,
    total_recv,
):
    t = lax.axis_index("ta")
    ha = lax.axis_index("ha")
    wa = lax.axis_index("wa")
    core = lax.rem(ha, 2)
    x = (ha // 2) * 2 + wa // 4
    y = lax.rem(wa, 4)

    def at(z, xx, cc, yy):
        return (z, (xx // 2) * 2 + cc, lax.rem(xx, 2) * 4 + yy)

    def near(dt, dh, dw):
        return (wrap(t + dt, 8), wrap(ha + dh, 4), wrap(wa + dw, 8))

    around = [(dh, dw) for dh in (-1, 0, 1) for dw in (-1, 0, 1) if (dh, dw) != (0, 0)]
    partners = [near(dt, dh, dw) for dt in (-1, 0, 1) for dh, dw in around]
    partners += [at(t, x, 1 - core, y)]
    partners += [at(t, wrap(x + k, 4), core, y) for k in (1, 2, 3)]
    partners += [at(t, x, core, wrap(y + k, 4)) for k in (1, 2, 3)]
    partners += [near(k, 0, 0) for k in range(1, 8)]
    barrier = pltpu.get_barrier_semaphore()
    for device in partners:
        pl.semaphore_signal(barrier, inc=1, device_id=device, device_id_type=MESH)

    loads = [
        pltpu.make_async_copy(far, here, load_sem.at[n])
        for n, (far, here) in enumerate(((feat_hbm, feat), (cot_hbm, cot), (weight_hbm, weight), (gain_hbm, gain)))
    ]
    for load in loads:
        load.start()

    def ones(condition):
        return jnp.where(condition, 1.0, 0.0).astype(BF16)

    line = lax.broadcasted_iota(jnp.int32, (96, 1024), 0)
    cell = lax.broadcasted_iota(jnp.int32, (96, 1024), 1)
    first_column = jnp.where(line < 64, line * 16, (line & 15) * 256 + jnp.where(line < 80, 240, 0))
    usable = (line < 64) | ((line & 15) < 4)
    select[0] = ones(usable & (cell == first_column + 15))
    select[1] = ones(usable & (cell == first_column))
    loads[3].wait()
    loads[0].wait()

    @pl.loop(0, 16)
    def _(n):
        rows = pl.ds(pl.multiple_of(n * 64, 64), 64)
        normed = normalise(feat[rows, :], gain[...])[3]
        act[2 + n // 4, pl.ds(pl.multiple_of(lax.rem(n, 4) * 64 + 16, 16), 64), :] = (
            normed * jax.nn.sigmoid(normed)
        ).astype(BF16)

    for n in range(2):
        for side in range(2):
            unused = pl.ds(32 * n, 32)
            halo_t[n, side, unused] = jnp.zeros((32, 256), BF16)

    pl.semaphore_wait(barrier, len(partners))

    def rows_of(ref, frame, frames, row, rows):
        return ref.at[pl.ds(frame, frames), pl.ds(row * 16, rows * 16), :]

    frame_moves = []
    row_moves = []
    column_moves = []
    for n, (ref, dt, own, ends) in enumerate(((act, 1, 2, ((5, 1), (4, 0))), (grd, -1, 0, ((0, 4), (1, 5))))):
        at_sem = iter(range(18))

        def move(source, target, device):
            m = next(at_sem)
            return remote(source, target, halo_send.at[n, m], halo_recv.at[n, m], device)

        frame_moves.append(
            [
                move(
                    rows_of(ref, a, 1, 1, 16) if n == 0 else cot.at[pl.ds(a * 256, 256)].reshape(1, 256, 256),
                    rows_of(ref, b, 1, 1, 16),
                    near(dt, 0, 0),
                )
                for a, b in ends
            ]
        )
        (a0, b0), (a1, b1) = ends
        a, b = min(a0, a1), min(b0, b1)
        row_moves.append(
            [
                [
                    move(rows_of(ref, source, count, row, 1), rows_of(ref, target, count, row - 16 * dh, 1), near(d, dh, 0))
                    for dh, row in ((1, 16), (-1, 1))
                ]
                for d, source, target, count in ((0, own, own, 4), (dt, a, b, 2))
            ]
        )
        column_moves.append(
            [
                [
                    move(edge.at[n, side, pl.ds(begin, count)], borders.at[n, side, pl.ds(begin, count)], near(d, dh, dw))
                    for side, dw in ((0, 1), (1, -1))
                    for begin, count, dh in (main, (64, 16, 1), (80, 16, -1))
                ]
                for d, borders, main in ((0, halo, (0, 64, 0)), (dt, halo_t, ((a - own) * 16, 32, 0)))
            ]
        )

    def start(copies):
        for copy in copies:
            copy.start()

    def take(copies):
        for copy in copies:
            copy.wait_recv()

    def edges(n, own):
        for side in range(2):
            acc = None
            for f in range(4):
                term = dot(select[side, :, f * 256 : f * 256 + 256], own[f][...])
                acc = term if acc is None else acc + term
            edge[n, side] = acc.astype(BF16)

    start(frame_moves[0][:1])
    loads[1].wait()
    start(frame_moves[1][:1])
    start(row_moves[0][0] + row_moves[0][1])
    edges(0, [act.at[n + 2, 16:272] for n in range(4)])
    start(column_moves[0][0] + column_moves[0][1])

    for n in range(4):
        grd[n, 16:272, :] = cot[n * 256 : n * 256 + 256, :]
    start(frame_moves[0][1:])
    start(row_moves[1][0] + row_moves[1][1])
    edges(1, [cot.at[n * 256 : n * 256 + 256] for n in range(4)])
    start(column_moves[1][0] + column_moves[1][1])
    start(frame_moves[1][1:])
    for n in range(4):
        line = lax.broadcasted_iota(jnp.int32, (ROW, 96), 1)
        cell = lax.broadcasted_iota(jnp.int32, (ROW, 96), 0)
        row = jnp.where(line < 64, (line & 15) + 1, jnp.where(line < 80, 0, 17))
        frame = jnp.where(line < 64, line // 16, line & 15)
        put[0, n] = ones((frame == n) & (cell == row * 16))
        put[1, n] = ones((frame == n) & (cell == row * 16 + 15))
    cell = lax.broadcasted_iota(jnp.int32, (ROW, ROW), 0)
    other = lax.broadcasted_iota(jnp.int32, (ROW, ROW), 1)
    column = cell & 15
    shift[0] = ones((cell == other + 1) & (column != 0))
    shift[1] = ones((cell == other - 1) & (column != 15))

    for n in range(4):
        cot_t[n] = cot[n * 256 : (n + 1) * 256, :].T
    mixed[...] = jnp.zeros_like(mixed)
    back[...] = jnp.zeros_like(back)

    def clear(n, ref, borders, begin, frames):
        @pl.when(ha == 0)
        def _():
            for frame in range(frames):
                ref[begin + frame, 0:16, :] = jnp.zeros((16, 256), BF16)
            for side in range(2):
                borders[n, side, 64:80] = jnp.zeros((16, 256), BF16)

        @pl.when(ha == 3)
        def _():
            for frame in range(frames):
                ref[begin + frame, 272:288, :] = jnp.zeros((16, 256), BF16)
            for side in range(2):
                borders[n, side, 80:96] = jnp.zeros((16, 256), BF16)

        @pl.when(wa == 0)
        def _():
            borders[n, 0] = jnp.zeros((96, 256), BF16)

        @pl.when(wa == 7)
        def _():
            borders[n, 1] = jnp.zeros((96, 256), BF16)

    def clear_frame(ref, frame, at_end):
        @pl.when(at_end)
        def _():
            ref[frame] = jnp.zeros((ROW, 256), BF16)

    def take_near(n, ref, own):
        take(row_moves[n][0] + column_moves[n][0])
        clear(n, ref, halo, own, 4)

    def take_far(n, ref, far, at_end):
        take(row_moves[n][1] + column_moves[n][1])
        clear(n, ref, halo_t, far, 2)

        @pl.when(at_end)
        def _():
            for side in range(2):
                halo_t[n, side] = jnp.zeros((96, 256), BF16)

    def widen(n, ref, wide, frame, own, borders):
        rows = pl.ds(pl.multiple_of(frame * ROW, 16), ROW)
        wide[rows, 256:512] = ref[frame]
        for side, lanes in ((0, 0), (1, 512)):
            moved = dot(shift[side], ref[frame]) + dot(put[side, own], borders[n, side])
            wide[rows, lanes : lanes + 256] = moved.astype(BF16)

    take_near(0, act, 2)

    @pl.loop(0, 4)
    def _(frame):
        widen(0, act, act3, frame + 2, frame, halo)

    def to_pair(s):
        return remote(
            part.at[s, :, 1 - core], pair.at[s], pair_sem.at[0, s], pair_sem.at[1, s], at(t, x, 1 - core, y)
        )

    def along(half, k):
        return at(t, wrap(x + k, 4), core, y) if half == 0 else at(t, x, core, wrap(y + k, 4))

    def copy1(s, half, k):
        slot = wrap((x if half == 0 else y) + k, 4)
        return remote(
            send1.at[s, half, slot],
            recv1.at[s, half, k - 1],
            send1_sem.at[s, half, k - 1],
            recv1_sem.at[s, half, k - 1],
            along(half, k),
        )

    def copy2(s, half, k):
        slot = wrap((y if half == 0 else x) + k, 4)
        return remote(
            send2.at[s, half, slot],
            recv2.at[s, half, k - 1],
            send2_sem.at[s, half, k - 1],
            recv2_sem.at[s, half, k - 1],
            along(1 - half, k),
        )

    def stage_gradient(s):
        i, j = 2 - s // 3, lax.rem(s, 3)
        acc = None
        for n in range(4):
            frame, pairs = n + i, n
            if n == 0:
                frame, pairs = jnp.where(i == 0, 4, i), jnp.where(i == 0, 4, 0)
            rows = pl.ds(pl.multiple_of(frame * ROW + j * 16, 16), 256)
            term = dot(cot_t[pairs], act3[rows, :])
            acc = term if acc is None else acc + term
        part[s] = acc.reshape(2, 2, 64, 768)
        to_pair(s).start()

    def stage_first(s):
        to_pair(s).wait_recv()
        for n in range(2):
            pair[s, n] = pair[s, n] + part[s, n, core]
        for d in range(4):
            n, r = d // 2, (d % 2) * 32
            send1[s, 0, d] = pair[s, n, r : r + 32, 0:384].astype(BF16)
            rows = [pair[s, e // 2, (e % 2) * 32 + d * 8 : (e % 2) * 32 + d * 8 + 8, 384:768] for e in range(4)]
            send1[s, 1, d] = jnp.concatenate(rows, axis=0).astype(BF16)
        for k in (2, 1, 3):
            for half in range(2):
                copy1(s, half, k).start()

    def stage_second(s):
        for half in range(2):
            for k in (1, 2, 3):
                copy1(s, half, k).wait_recv()
        own = pair[s, x // 2, pl.ds(pl.multiple_of(lax.rem(x, 2) * 32, 32), 32), 0:384]
        for k in range(3):
            own = own + recv1[s, 0, k].astype(F32)
        mid[s, 0] = own.reshape(4, 8, 384)
        send2[s, 0] = own.reshape(4, 8, 384).astype(BF16)
        rows = [
            pair[s, e // 2, pl.ds(pl.multiple_of((e % 2) * 32 + y * 8, 8), 8), 384:768] for e in range(4)
        ]
        own = jnp.concatenate(rows, axis=0)
        for k in range(3):
            own = own + recv1[s, 1, k].astype(F32)
        mid[s, 1] = own.reshape(4, 8, 384)
        send2[s, 1] = own.reshape(4, 8, 384).astype(BF16)
        for k in (2, 1, 3):
            for half in range(2):
                copy2(s, half, k).start()

    def owner_of(s, tile):
        return lax.rem(6 * s + tile, 8)

    def owned(s):
        return lax.rem(t + 2 * s, 8)

    def to_owner(s, tile):
        owner = owner_of(s, tile)
        k = wrap(t - owner - 1, 8)
        return remote(flat.at[s, tile], recv3.at[s, k], flat_sem.at[s, tile], recv3_sem.at[s, k], (owner, ha, wa))

    def from_owner(s, tile, k):
        place = total.at[s, tile]
        return remote(place, place, total_send.at[s, k - 1], total_recv.at[s, tile], near(k, 0, 0))

    def to_every(s, k):
        place = every.at[s - OWNED, t]
        return remote(place, place, every_send.at[s - OWNED, k - 1], every_recv.at[s - OWNED, t], near(k, 0, 0))

    def second_sums(s):
        for half in range(2):
            for k in (1, 2, 3):
                copy2(s, half, k).wait_recv()
        sums = []
        for half, slot in ((0, y), (1, x)):
            own = mid[s, half, slot]
            for k in range(3):
                own = own + recv2[s, half, k].astype(F32)
            sums.append(own)
        return sums

    def stage_third(s):
        sums = second_sums(s)
        for half in range(2):
            for k in range(3):
                flat[s, half * 3 + k] = sums[half][:, k * 128 : k * 128 + 128]
        for tile in range(6):

            @pl.when(t != owner_of(s, tile))
            def _():
                to_owner(s, tile).start()

    def stage_every(n):
        s = n + OWNED
        sums = second_sums(s)
        for half in range(2):
            every[n, t, :, half * 384 : half * 384 + 384] = sums[half].astype(BF16)
        for k in (4, 3, 5, 2, 6, 1, 7):
            to_every(s, k).start()

    def stage_owner(s):
        tile = owned(s)

        @pl.when(tile < 6)
        def _():
            own = flat[s, tile]
            for k in range(7):
                remote(
                    flat.at[s, 0], recv3.at[s, k], flat_sem.at[s, 0], recv3_sem.at[s, k], near(1, 0, 0)
                ).wait_recv()
                own = own + recv3[s, k]
            total[s, tile] = own * scale
            for k in (4, 3, 5, 2, 6, 1, 7):
                from_owner(s, tile, k).start()

    def stage_weight(_):
        loads[2].wait()

    def stage_mixed(s):
        i, j = 2 - s // 3, lax.rem(s, 3)
        for n in range(4):
            rows = pl.ds(pl.multiple_of((n + i) * ROW + j * 16, 16), 256)
            mixed[n * 256 : n * 256 + 256, :] += dot(act3[rows, :], weight[i * 3 + j])

    def stage_back(s):
        i, j = 2 - s // 3, lax.rem(s, 3)
        for n in range(4):
            rows = pl.ds(pl.multiple_of((n + 2 - i) * ROW + (2 - j) * 16, 16), 256)
            acc = None
            for k in range(3):
                term = lax.dot_general(
                    grd3[rows, (2 - k) * 256 : (3 - k) * 256],
                    weight[i * 3 + j, k * 256 : k * 256 + 256, :],
                    (((1,), (1,)), ((), ())),
                    preferred_element_type=F32,
                )
                acc = term if acc is None else acc + term
            back[n * 256 : n * 256 + 256, :] += acc

    def stage_act(_):
        take_far(0, act, 0, t == 0)
        take(frame_moves[0][:1])
        clear_frame(act, 1, t == 0)
        widen(0, act, act3, 1, 3, halo_t)
        take(frame_moves[1][:1])
        cot_t[4] = grd[4, 16:272, :].T

        @pl.when(t == 7)
        def _():
            cot_t[4] = jnp.zeros((256, 256), BF16)


    def stage_act_last(_):
        take(frame_moves[0][1:])
        clear_frame(act, 0, t == 0)
        widen(0, act, act3, 0, 2, halo_t)

    def stage_cot_near(_):
        take_near(1, grd, 0)

    def stage_cot(frame):
        widen(1, grd, grd3, frame, frame, halo)

    def stage_cot_late(_):
        take_far(1, grd, 4, t == 7)
        take(frame_moves[1][1:])
        for frame in (4, 5):
            clear_frame(grd, frame, t == 7)
        for frame in range(2):
            widen(1, grd, grd3, frame + 4, frame, halo_t)

    def stage_decoded(n):
        for m in range(4):
            rows = pl.ds(pl.multiple_of(n * 256 + m * 64, 64), 64)
            decoded[rows, :] = (feat[rows, :].astype(F32) + mixed[rows, :]).astype(BF16)

    def stage_grad(n):
        @pl.loop(0, 4)
        def _(m):
            rows = pl.ds(pl.multiple_of(n * 256 + m * 64, 64), 64)
            _, inverse, unit, normed = normalise(feat[rows, :], gain[...])
            logistic = jax.nn.sigmoid(normed)
            grad_unit = back[rows, :] * logistic * (1.0 + normed * (1.0 - logistic)) * gain[...]
            grad = inverse * (grad_unit - unit * jnp.mean(grad_unit * unit, axis=-1, keepdims=True))
            grad_feat[rows, :] = (cot[rows, :].astype(F32) + grad).astype(BF16)

    plan = (
        (stage_act, 3, 1, 1, 1),
        (stage_gradient, 0, 1, 1, SLABS),
        (stage_first, 2, 1, 1, SLABS),
        (stage_second, 8, 1, 1, SLABS),
        (stage_third, 13, 1, 1, OWNED),
        (stage_every, 21, 1, 1, SLABS - OWNED),
        (stage_owner, 20, 1, 1, OWNED),
        (stage_weight, 11, 1, 1, 1),
        (stage_cot_near, 9, 1, 1, 1),
        (stage_cot, 12, 1, 1, 4),
        (stage_act_last, 16, 1, 1, 1),
        (stage_cot_late, 17, 1, 1, 1),
        (stage_mixed, 11, 1, 1, SLABS),
        (stage_back, 20, 1, 1, SLABS),
        (stage_decoded, 21, 2, 1, 4),
        (stage_grad, 30, 1, 1, 4),
    )

    @pl.loop(0, TICKS)
    def _(tick):
        for stage, begin, over, under, count in plan:
            past = tick - begin
            n = (jnp.maximum(past, 0) * under + over - 1) // over

            @pl.when((past >= 0) & (n < count) & ((n * over) // under == past))
            def _():
                stage(n)

    @pl.loop(0, SLABS)
    def _(s):
        to_pair(s).wait_send()
        for half in range(2):
            for k in (1, 2, 3):
                copy1(s, half, k).wait_send()
                copy2(s, half, k).wait_send()

    def taps(s):
        return (2 - s // 3) * 9 + lax.rem(s, 3) * 3

    @pl.loop(0, OWNED)
    def _(s):
        for tile in range(6):

            @pl.when(t != owner_of(s, tile))
            def _():
                to_owner(s, tile).wait_send()
                from_owner(s, tile, 1).wait_recv()

        @pl.when(owned(s) < 6)
        def _():
            for k in range(1, 8):
                from_owner(s, 0, k).wait_send()

        for k in range(3):
            for n in range(2):
                grad_weight[taps(s) + k, :, n * 128 : n * 128 + 128] = total[s, k * 2 + n]

    @pl.loop(OWNED, SLABS)
    def _(s):
        n = s - OWNED
        for k in range(1, 8):
            place = every.at[n, wrap(t + k, 8)]
            remote(place, place, every_send.at[n, k - 1], every_recv.at[n, wrap(t + k, 8)], near(k, 0, 0)).wait_recv()
        own = every[n, 0].astype(F32)
        for z in range(1, 8):
            own = own + every[n, z].astype(F32)
        own = own * scale
        for k in range(3):
            grad_weight[taps(s) + k] = own[:, k * 256 : k * 256 + 256]
        for k in range(1, 8):
            to_every(s, k).wait_send()

    for n in range(2):
        for copy in frame_moves[n] + sum(row_moves[n] + column_moves[n], []):
            copy.wait_send()


def finish(*refs):
    copies = [pltpu.make_async_copy(refs[n], refs[n + 3], refs[6].at[n]) for n in range(3)]
    for copy in copies:
        copy.start()
    for copy in copies:
        copy.wait()


def body(features, norm_gain, conv_weight, cotangent):
    frames, height, width, channels = features.shape
    cells = frames * height * width
    owners = lax.axis_size("ha") * lax.axis_size("wa")
    voxels = cells * owners * lax.axis_size("ta")
    vmem = pl.BlockSpec(memory_space=pltpu.VMEM)
    hbm = pl.BlockSpec(memory_space=pltpu.HBM)
    anywhere = pl.BlockSpec(memory_space=pl.ANY)
    dma = pltpu.SemaphoreType.DMA

    def run(*refs):
        kernel(float(voxels) ** (-0.5), *refs)

    results = (
        jax.ShapeDtypeStruct((cells, channels), BF16),
        jax.ShapeDtypeStruct((cells, channels), BF16),
        jax.ShapeDtypeStruct((27, channels // owners, channels), F32),
    )
    held = pl.pallas_call(
        run,
        out_shape=results,
        in_specs=[hbm] * 4,
        out_specs=(vmem, vmem, vmem),
        scratch_shapes=[
            pltpu.VMEM((1, 256), F32),
            pltpu.VMEM((1024, 256), BF16),
            pltpu.VMEM((1024, 256), BF16),
            pltpu.VMEM((6, ROW, 256), BF16),
            pltpu.VMEM((6, ROW, 256), BF16),
            pltpu.VMEM((PADDED, 768), BF16),
            pltpu.VMEM((PADDED, 768), BF16),
            pltpu.VMEM((5, 256, 256), BF16),
            pltpu.VMEM((SLABS, 768, 256), BF16),
            pltpu.VMEM((2, 96, 1024), BF16),
            pltpu.VMEM((2, 4, ROW, 96), BF16),
            pltpu.VMEM((2, ROW, ROW), BF16),
            pltpu.VMEM((2, 2, 96, 256), BF16),
            pltpu.VMEM((2, 2, 96, 256), BF16),
            pltpu.VMEM((2, 2, 96, 256), BF16),
            pltpu.VMEM((1024, 256), F32),
            pltpu.VMEM((1024, 256), F32),
            pltpu.VMEM((SLABS, 2, 2, 64, 768), F32),
            pltpu.VMEM((SLABS, 2, 64, 768), F32),
            pltpu.VMEM((SLABS, 2, 4, 32, 384), BF16),
            pltpu.VMEM((SLABS, 2, 3, 32, 384), BF16),
            pltpu.VMEM((SLABS, 2, 4, 8, 384), F32),
            pltpu.VMEM((SLABS, 2, 4, 8, 384), BF16),
            pltpu.VMEM((SLABS, 2, 3, 8, 384), BF16),
            pltpu.VMEM((OWNED, 6, 8, 128), F32),
            pltpu.VMEM((OWNED, 7, 8, 128), F32),
            pltpu.VMEM((SLABS - OWNED, 8, 8, 768), BF16),
            pltpu.VMEM((SLABS, 6, 8, 128), F32),
            dma((4,)),
            dma((2, 18)),
            dma((2, 18)),
            dma((2, SLABS)),
            dma((SLABS, 2, 3)),
            dma((SLABS, 2, 3)),
            dma((SLABS, 2, 3)),
            dma((SLABS, 2, 3)),
            dma((OWNED, 6)),
            dma((OWNED, 7)),
            dma((SLABS - OWNED, 7)),
            dma((SLABS - OWNED, 8)),
            dma((OWNED, 7)),
            dma((OWNED, 6)),
        ],
        compiler_params=pltpu.CompilerParams(
            collective_id=0, has_side_effects=True, vmem_limit_bytes=52 << 20
        ),
    )(
        *(
            pltpu.with_memory_space_constraint(array, pltpu.HBM)
            for array in (
                features.reshape(cells, channels),
                norm_gain.reshape(1, channels),
                conv_weight.reshape(9, 3 * channels, channels),
                cotangent.reshape(cells, channels),
            )
        ),
    )
    decoded, grad_features, grad_weight = pl.pallas_call(
        finish,
        out_shape=results,
        in_specs=[anywhere] * 3,
        out_specs=[hbm] * 3,
        scratch_shapes=[dma((3,))],
        compiler_params=pltpu.CompilerParams(vmem_limit_bytes=4 << 20),
    )(*held)
    grad_weight = grad_weight.reshape(3, 3, 3, channels // owners, channels).transpose(0, 1, 2, 4, 3)
    return decoded.reshape(features.shape), grad_features.reshape(features.shape), grad_weight


def solution(mesh):
    placed = (P("ta", "ha", "wa", None), P(), P(), P("ta", "ha", "wa", None))
    return jax.shard_map(
        body,
        mesh=mesh,
        in_specs=placed,
        out_specs=(
            P("ta", "ha", "wa", None),
            P("ta", "ha", "wa", None),
            P(None, None, None, None, ("ha", "wa")),
        ),
        check_vma=False,
    )
```
